32 devices in a mesh: seq: 8 (over z, x), row: 4 (over y, core).
Axes of the slice: x: 2, y: 2, z: 4, core: 2. Of those that a mesh axis runs over, the one named last changes fastest.
Arguments:
- tokens: bfloat16 [8192, 1536], P(('seq', 'row')), may hold values from -6 to 6
- routes: int32 [1, 8192, 8], P(None, ('seq', 'row')), may hold values from 0 to 19, all different within a row; in each aligned block of 256 rows (0 to 255, 256 to 511, ..., all dimensions but the last counted through in order) at most 128 rows name the same one
- attn_gain: float32 [1, 1536], replicated, may hold values from 0.5 to 1.5
- ffn_gain: float32 [1, 1536], replicated, may hold values from 0.5 to 1.5
- query_weight: bfloat16 [1, 1536, 1536], P(None, 'seq', 'row'), may hold values from -0.76546554 to 0.76546554
- keyval_weight: bfloat16 [1, 1536, 8, 128], P(None, 'seq', 'row'), may hold values from -0.76546554 to 0.76546554
- output_weight: bfloat16 [1, 1536, 1536], P(None, 'row', 'seq'), may hold values from -1.5 to 1.5
- router_weight: bfloat16 [1, 1536, 20], replicated, may hold values from -0.15625 to 0.15625
- expert_up: bfloat16 [1, 20, 1536, 1024], P(None, 'row', 'seq'), may hold values from -0.15625 to 0.15625
- expert_down: bfloat16 [1, 20, 512, 1536], P(None, 'row', None, 'seq'), may hold values from -0.75 to 0.75
- cotangent: bfloat16 [8192, 1536], P(('seq', 'row')), may hold values from -6 to 6
Outputs:
- result: bfloat16 [8192, 1536], P(('seq', 'row'))
- token_grad: float32 [8192, 1536], P(('seq', 'row'))
- attn_gain_grad: float32 [1, 1536], replicated
- ffn_gain_grad: float32 [1, 1536], replicated
- query_grad: float32 [1, 1536, 1536], P(None, 'seq', 'row')
- keyval_grad: float32 [1, 1536, 8, 128], P(None, 'seq', 'row')
- output_grad: float32 [1, 1536, 1536], P(None, 'row', 'seq')
- router_grad: float32 [1, 1536, 20], replicated
- expert_up_grad: float32 [1, 20, 1536, 1024], P(None, 'row', 'seq')
- expert_down_grad: float32 [1, 20, 512, 1536], P(None, 'row', None, 'seq')
The draws below stay inside these ranges and needn't reach their ends.
Inputs may be any that keep to these rules, and one draw needn't show every extreme that they name: `routes`: in each layer the 256 rows of one device name every expert at most 128 times; each row names 8 different experts.
All inputs are finite; a program needn't handle non-finite values.
Results may differ from the reference program's by a relative error of at most 0.028.
The reference program's roundings to bfloat16 on the way count: a program that leaves them out, or rounds other values in their place, can miss the bound.
Values may be sent and summed in bfloat16 or wider, within the bound.
No kernel may reach another device: no remote copies, remote signals or barrier semaphores. Data moves between devices by JAX's collectives and lax.ppermute only.
A program may use at most 256 MiB of HBM per device.

```python
import math
import jax
import jax.numpy as jnp
import numpy as np
from jax import lax

D = 1536
HEADS = 24
KVH = 8
HD = 64
FF = 512
TOP = 8
LAYERS = 1
TOK_DEV = 256
EXPERTS = 20
SEQ_LEN = 1024
TOKENS = 8192
CAP = 128


def draw_query_weight(key, part):
    drawn = jnp.clip(jax.random.normal(key, (LAYERS, D, HEADS, HD), jnp.float32), -6.0, 6.0) * D ** (-0.5)
    return drawn.reshape(LAYERS, D, HEADS * HD).astype(jnp.bfloat16)


def draw_keyval_weight(key, part):
    drawn = jnp.clip(jax.random.normal(key, (LAYERS, D, KVH, 2 * HD), jnp.float32), -6.0, 6.0) * D ** (-0.5)
    return drawn.astype(jnp.bfloat16)


def block_levels(stream_key, extent, shards, low, high):
    def one(position, shards_of):
        heights = jax.random.uniform(jax.random.fold_in(jax.random.fold_in(stream_key, 6), position), (shards_of,), jnp.float32, low / len(shards), high / len(shards))
        return jnp.repeat(jnp.exp(heights), extent[position] // shards_of).reshape((-1,) + (1,) * (len(extent) - position - 1))

    factor_of = one(*shards[0])
    for cut in shards[1:]:
        factor_of = factor_of * one(*cut)
    return factor_of


def shared_out(key, own, number, rows, number_of, top, most, slope):
    order = jax.random.permutation(key, number_of)
    packed, ordinary = shares(number_of, rows * top, most, slope, True), shares(number_of, rows * top, most, slope, False)
    places = jnp.arange(number_of)

    def named(tallies, offset_by):
        used = int((tallies > 0).sum())
        fixed = max(1, used // 4)
        moved = fixed + (places - fixed + offset_by * (used - fixed)) % max(1, number_of - fixed)
        return jnp.zeros((number_of,), jnp.int32).at[order[jnp.where(places < fixed, places, moved)]].set(jnp.asarray(tallies, jnp.int32))

    tallies = jnp.where(number % 4 == 0, named(packed, number // 4), named(ordinary, number - number // 4 - 1))
    mixed = jax.random.permutation(jax.random.fold_in(own, 3), number_of)
    source_of, receiver = mixed[0:number_of // 2 * 2:2], mixed[1:number_of // 2 * 2:2]
    slack = jnp.minimum(tallies[source_of] - 1, most - tallies[receiver]) // 2
    slack = jnp.where((source_of == order[0]) | (receiver == order[0]) | (tallies[receiver] == 0), 0, jnp.maximum(slack, 0))
    moved = jax.random.randint(jax.random.fold_in(own, 4), (number_of // 2,), 0, 1 << 20) % (slack + 1)
    tallies = tallies.at[source_of].add(-moved).at[receiver].add(moved)
    items = jnp.searchsorted(jnp.cumsum(tallies), jnp.arange(rows * top), side="right").astype(jnp.int32)
    table = items.reshape(top, rows).T
    table = table[jax.random.permutation(jax.random.fold_in(own, 1), rows)]
    offset_by = jax.random.randint(jax.random.fold_in(own, 2), (rows, 1), 0, top)
    return jnp.take_along_axis(table, (jnp.arange(top)[None, :] + offset_by) % top, axis=1)


def shares(count, total, most, skew, full):
    portions = [(1 << 20) // math.isqrt(standing ** skew) + 1 for standing in range(1, count + 1)]
    largest = most if full else min(most, max(-(-total // count), total * portions[0] // sum(portions)))
    least = 1 if total - largest >= count - 1 else 0
    counts, spare = [largest] + [least] * (count - 1), total - largest - least * (count - 1)
    while spare > 0:
        candidates = [i for i in range(1, count) if counts[i] < largest] or [i for i in range(1, count) if counts[i] < most]
        whole, remaining = sum([portions[i] for i in candidates]), spare
        for i in candidates:
            more = min(most - counts[i], max(1, remaining * portions[i] // whole), spare)
            counts[i] = counts[i] + more
            spare = spare - more
    return np.array(counts)


def bell_draw(stream_key, extent, width, bound, shards=(), held_as=jnp.bfloat16):
    level = block_levels(stream_key, extent, shards, -0.22, 0.18) if shards else 1.0
    values = jax.random.normal(stream_key, extent, jnp.float32) * width * level
    return jnp.minimum(jnp.maximum(values, -bound), bound).astype(held_as)


def setup_inputs(seed: int = 0) -> dict:
    arg_keys = jax.random.split(jax.random.key(seed), 12)
    tokens = bell_draw(arg_keys[0], (TOKENS, D), 1.0, 6.0, ((0, 32),))
    routes_keys = jax.random.split(jax.random.fold_in(arg_keys[1], 1), LAYERS * TOKENS // TOK_DEV)
    routes_turns = jax.random.permutation(jax.random.fold_in(arg_keys[1], 3), LAYERS * TOKENS // TOK_DEV)
    routes = jax.vmap(lambda own, number: shared_out(jax.random.fold_in(arg_keys[1], 2), own, number, TOK_DEV, EXPERTS, TOP, CAP, 2))(routes_keys, routes_turns).reshape((LAYERS, TOKENS, TOP))
    attn_gain = jnp.clip(1.0 + 0.1 * jax.random.normal(arg_keys[2], (LAYERS, D), jnp.float32), 0.5, 1.5)
    ffn_gain = jnp.clip(1.0 + 0.1 * jax.random.normal(arg_keys[3], (LAYERS, D), jnp.float32), 0.5, 1.5)
    query_weight = draw_query_weight(jax.random.fold_in(arg_keys[11], 71), 0)
    keyval_weight = draw_keyval_weight(jax.random.fold_in(arg_keys[11], 71), 0)
    output_weight = bell_draw(arg_keys[6], (LAYERS, HEADS * HD, D), (HD // 4) ** -0.5, 1.5, ((1, 4), (2, 8)))
    router_weight = bell_draw(arg_keys[7], (LAYERS, D, EXPERTS), D ** -0.5, 0.15625)
    expert_up = bell_draw(arg_keys[8], (LAYERS, EXPERTS, D, 2 * FF), D ** -0.5, 0.15625, ((1, 4), (2, 8)))
    expert_down = bell_draw(arg_keys[9], (LAYERS, EXPERTS, FF, D), (FF // 8) ** -0.5, 0.75, ((1, 4), (3, 8)))
    cotangent = bell_draw(arg_keys[10], (TOKENS, D), 1.0, 6.0, ((0, 32),))
    return {"tokens": tokens, "routes": routes, "attn_gain": attn_gain, "ffn_gain": ffn_gain, "query_weight": query_weight, "keyval_weight": keyval_weight, "output_weight": output_weight, "router_weight": router_weight, "expert_up": expert_up, "expert_down": expert_down, "cotangent": cotangent}


@jax.custom_vjp
def low(v):
    return lax.optimization_barrier(v.astype(jnp.bfloat16)).astype(jnp.float32)

@jax.custom_vjp
def low_back(v):
    return v

def low_keep(v):
    return (low(v), None)

def low_pass(kept, grad):
    return (grad,)

def back_keep(v):
    return (v, None)

def back_low(kept, grad):
    return (low(grad),)
low.defvjp(low_keep, low_pass)
low_back.defvjp(back_keep, back_low)
precise = lax.Precision.HIGHEST
epsilon = 1e-06

def rms_norm(features, norm_gain):
    inverse_rms = lax.rsqrt(lax.optimization_barrier(jnp.mean(features * features, axis=-1, keepdims=True)) + epsilon)
    return features * inverse_rms * norm_gain

def rotary_tables(seq_length, head_width):
    half_width = head_width // 2
    inverse_freq = 10000.0 ** (-jnp.arange(half_width, dtype=jnp.float32) * 2.0 / head_width)
    angles = jnp.arange(seq_length, dtype=jnp.float32)[:, None] * inverse_freq[None, :]
    return (jnp.cos(angles), jnp.sin(angles))

def rotate(arrays, cosine_table, sine_table):
    half_width = arrays.shape[-1] // 2
    cosine_wide = cosine_table[:, None, :]
    sine_wide = sine_table[:, None, :]
    first_half = arrays[..., :half_width]
    second_half = arrays[..., half_width:]
    return jnp.concatenate([first_half * cosine_wide - second_half * sine_wide, second_half * cosine_wide + first_half * sine_wide], axis=-1)

def attend_sequence(inputs):
    queries, key_rows, value_rows = inputs
    seq_length = queries.shape[0]
    group_size = queries.shape[1] // key_rows.shape[1]
    keys_wide = jnp.repeat(key_rows, group_size, axis=1)
    values_wide = jnp.repeat(value_rows, group_size, axis=1)
    scores = jnp.einsum('qhd,khd->hqk', queries, keys_wide, precision=precise) * HD ** (-0.5)
    scores = low_back(scores)
    positions = jnp.arange(seq_length, dtype=jnp.int32)
    scores = jnp.where(positions[:, None] >= positions[None, :], scores, -1e+30)
    maximum = lax.optimization_barrier(jnp.max(scores, axis=-1, keepdims=True))
    exponent = jnp.exp(scores - maximum)
    weights = exponent / lax.optimization_barrier(jnp.sum(exponent, axis=-1, keepdims=True))
    return jnp.einsum('hqk,khd->qhd', low(weights), values_wide, precision=precise)

def attention_block(hidden, norm_gain, query_weight, keyval_weight, output_weight, cosine_table, sine_table):
    batch_count, seq_length = (hidden.shape[0], hidden.shape[1])
    normed = low(rms_norm(hidden, norm_gain))
    queries = low_back(jnp.einsum('bsd,de->bse', normed, query_weight, precision=precise))
    queries = low(rotate(queries.reshape(batch_count, seq_length, HEADS, HD), cosine_table, sine_table))
    keyval = low_back(jnp.einsum('bsd,dkf->bskf', normed, keyval_weight, precision=precise))
    key_rows = low(rotate(keyval[..., :HD], cosine_table, sine_table))
    value_rows = low(keyval[..., HD:])
    attended = lax.map(jax.checkpoint(attend_sequence), (queries, key_rows, value_rows))
    attended = low(low_back(attended.reshape(batch_count, seq_length, HEADS * HD)))
    return hidden + low_back(jnp.einsum('bse,ed->bsd', attended, output_weight, precision=precise))

def slot_table(route_ids):
    flat_ids = route_ids.reshape(-1)
    member = (flat_ids[:, None] == jnp.arange(EXPERTS, dtype=jnp.int32)[None, :]).astype(jnp.int32)
    ranks = lax.optimization_barrier(jnp.sum((jnp.cumsum(member, axis=0) - member) * member, axis=1)).astype(jnp.int32)
    total_slots = flat_ids.shape[0]
    room = TOKENS // TOK_DEV * CAP
    table = jnp.full((EXPERTS, room), total_slots, dtype=jnp.int32)
    return table.at[flat_ids, ranks].set(jnp.arange(total_slots, dtype=jnp.int32))

def expert_block(hidden, norm_gain, router_weight, expert_up, expert_down, route_ids, table):
    flat_hidden = hidden.reshape(-1, D)
    normed = low(rms_norm(flat_hidden, norm_gain))
    logits = low_back(jnp.dot(normed, router_weight, precision=precise))
    chosen = jnp.take_along_axis(logits, route_ids, axis=1)
    mixing = jax.nn.softmax(chosen, axis=-1).reshape(-1)
    total_slots = mixing.shape[0]

    def one_expert(moe_sum, inputs):
        slot_ids, up_matrix, down_matrix = inputs
        valid = slot_ids < total_slots
        safe_ids = jnp.minimum(slot_ids, total_slots - 1)
        token_ids = safe_ids // TOP
        rows_in = low_back(normed[token_ids])
        up_out = low_back(jnp.dot(rows_in, up_matrix, precision=precise))
        active = low(jax.nn.silu(up_out[:, :FF]) * up_out[:, FF:])
        produced = low(low_back(jnp.dot(active, down_matrix, precision=precise)))
        share = jnp.where(valid, mixing[safe_ids], 0.0)
        return (moe_sum.at[token_ids].add(share[:, None] * produced), None)
    moe_sum, _ = lax.scan(jax.checkpoint(one_expert), jnp.zeros_like(flat_hidden), (table, expert_up, expert_down))
    return hidden + moe_sum.reshape(hidden.shape)

def forward(tokens, attn_gain, ffn_gain, query_weight, keyval_weight, output_weight, router_weight, expert_up, expert_down, routes, tables):
    hidden = tokens.reshape(TOKENS // SEQ_LEN, SEQ_LEN, D)
    cosine_table, sine_table = rotary_tables(SEQ_LEN, HD)
    for layer_index in range(LAYERS):
        hidden = attention_block(hidden, attn_gain[layer_index], query_weight[layer_index], keyval_weight[layer_index], output_weight[layer_index], cosine_table, sine_table)
        hidden = expert_block(hidden, ffn_gain[layer_index], router_weight[layer_index], expert_up[layer_index], expert_down[layer_index], routes[layer_index], tables[layer_index])
    return hidden.reshape(TOKENS, D)

def reference(tokens, routes, attn_gain, ffn_gain, query_weight, keyval_weight, output_weight, router_weight, expert_up, expert_down, cotangent):
    tables = jnp.stack([slot_table(routes[layer_index]) for layer_index in range(LAYERS)])
    floats = tuple((array.astype(jnp.float32) for array in (tokens, attn_gain, ffn_gain, query_weight, keyval_weight, output_weight, router_weight, expert_up, expert_down)))

    def run(*arrays):
        return forward(*arrays, routes, tables)
    output, pullback = jax.vjp(run, *floats)
    grads = pullback(cotangent.astype(jnp.float32))
    return (output.astype(jnp.bfloat16), grads[0], grads[1], grads[2], grads[3], grads[4], grads[5], grads[6], grads[7], grads[8])
```

```python
import functools

import jax
import jax.numpy as jnp
from jax import lax
from jax.experimental import pallas as pl
from jax.experimental.pallas import tpu as pltpu
from jax.sharding import PartitionSpec as P

epsilon = 1e-06
outer_count = 4
pair_count = 2
bf16 = jnp.bfloat16
f32 = jnp.float32


def inverse_rms(features):
    return lax.rsqrt(jnp.mean(features * features, axis=-1, keepdims=True) + epsilon)


def rotary_tables(seq_length, head_width):
    half_width = head_width // 2
    inverse_freq = 10000.0 ** (-jnp.arange(half_width, dtype=f32) * 2.0 / head_width)
    angles = jnp.arange(seq_length, dtype=f32)[:, None] * inverse_freq[None, :]
    return (jnp.cos(angles), jnp.sin(angles))


transposed = (((1,), (1,)), ((), ()))


def half_swap(x):
    lane = lax.broadcasted_iota(jnp.int32, x.shape, 1)
    return jnp.where(lane % 64 < 32, pltpu.roll(x, 96, 1), pltpu.roll(x, 32, 1))


def line_dot(rows, line_refs):
    part = rows.shape[1] // len(line_refs)
    total = 0.0
    for index, ref in enumerate(line_refs):
        total = total + jnp.dot(
            rows[:, index * part : (index + 1) * part], ref[...], preferred_element_type=f32
        )
    return total


def attend_forward_kernel(lines, heads, group, block, together, *refs):
    x_ref, cos_ref, sin_ref = refs[:3]
    qkv_refs, out_refs = refs[3 : 3 + lines], refs[3 + lines : 3 + 2 * lines]
    q_ref, k_ref, v_ref, kt_ref, o_ref, low_ref, sum_ref, part_ref = refs[
        3 + 2 * lines : 11 + 2 * lines
    ]
    keys, values = refs[11 + 2 * lines :]
    tiles = (heads + 1) // 2
    kv_count = heads // group
    step = pl.program_id(0)
    here = pl.multiple_of(step * block, block)
    cosine, sine = cos_ref[...], sin_ref[...]
    lane = lax.broadcasted_iota(jnp.int32, cosine.shape, 1)
    first = lane < 64
    projected = line_dot(x_ref[...], qkv_refs)
    query_tiles = []
    for tile in range(tiles):
        part = projected[:, tile * 128 : (tile + 1) * 128]
        part = (part * cosine + half_swap(part) * sine).astype(bf16) * bf16(0.125)
        q_ref[:, tile * 128 : (tile + 1) * 128] = part
        query_tiles.append(part)
    for kv in range(kv_count):
        part = projected[:, (tiles + kv) * 128 : (tiles + kv + 1) * 128]
        part = jnp.where(first, part * cosine + half_swap(part) * sine, part)
        turned = pltpu.roll(part, 64, 1)
        key_wide = jnp.where(first, part, turned)
        value_wide = jnp.where(first, turned, part)
        columns = slice(kv * 128, (kv + 1) * 128)
        k_ref[:, columns] = key_wide.astype(bf16)
        v_ref[:, columns] = value_wide.astype(bf16)
        both = part.T.astype(bf16)
        kt_ref[kv * 64 : (kv + 1) * 64, :] = both[:64]
        keys[pl.ds(here, block), columns] = key_wide.astype(bf16)
        values[kv * 64 : (kv + 1) * 64, pl.ds(here, block)] = both[64:]
    row = lax.broadcasted_iota(jnp.int32, (block, block), 0)
    column = lax.broadcasted_iota(jnp.int32, (block, block), 1)
    queries = []
    for head in range(heads):
        mine = first if head % 2 == 0 else jnp.logical_not(first)
        queries.append(jnp.where(mine, query_tiles[head // 2], bf16(0)))

    def scores_of(j, head):
        kv = slice(head // group * 128, (head // group + 1) * 128)
        key = keys[pl.ds(pl.multiple_of(j * block, block), block), kv]
        scores = lax.dot_general(key, queries[head], transposed, preferred_element_type=f32)
        return jnp.where(row + j * block <= column + here, scores, -1e30)

    outs = []
    for start in range(0, heads, together):
        some = range(start, min(start + together, heads))

        def stats(j, carry, some=some):
            after = []
            for head, (top, total) in zip(some, carry):
                scores = scores_of(j, head)
                new_top = jnp.maximum(top, jnp.max(scores, axis=0, keepdims=True))
                total = total * jnp.exp(top - new_top) + jnp.sum(
                    jnp.exp(scores - new_top), axis=0, keepdims=True
                )
                after.append((new_top, total))
            return after

        fresh = [(jnp.full((1, block), -1e30, f32), jnp.zeros((1, block), f32)) for _ in some]
        found = lax.fori_loop(0, step + 1, stats, fresh)
        for head, (top, total) in zip(some, found):
            sum_ref[head : head + 1, :] = top + jnp.log(total)
        scales = [(top, 1.0 / total) for top, total in found]

        def mix(j, carry, some=some, scales=scales):
            after = []
            for head, (top, inverse), sofar in zip(some, scales, carry):
                weights = (jnp.exp(scores_of(j, head) - top) * inverse).astype(bf16)
                kv = slice(head // group * 64, (head // group + 1) * 64)
                value = values[kv, pl.ds(pl.multiple_of(j * block, block), block)]
                after.append(sofar + jnp.dot(value, weights, preferred_element_type=f32))
            return after

        outs += lax.fori_loop(0, step + 1, mix, [jnp.zeros((64, block), f32) for _ in some])
    if heads % 2:
        outs.append(jnp.zeros((64, block), f32))
    for tile in range(tiles):
        both = jnp.concatenate(outs[tile * 2 : tile * 2 + 2], axis=0).T
        o_ref[:, tile * 128 : (tile + 1) * 128] = both
        low_ref[:, tile * 128 : (tile + 1) * 128] = both.astype(bf16)
    part = part_ref.shape[1] // lines
    for index, ref in enumerate(out_refs):
        part_ref[:, index * part : (index + 1) * part] = lax.dot_general(
            low_ref[...], ref[...], transposed, preferred_element_type=f32
        ).astype(bf16)


def attend_backward_kernel(lines, heads, group, block, together, *refs):
    g_ref, cos_ref, sin_ref = refs[:3]
    qkv_refs, out_refs = refs[3 : 3 + lines], refs[3 + lines : 3 + 2 * lines]
    q_ref, k_ref, v_ref, kt_ref, o_ref, sum_ref = refs[3 + 2 * lines : 9 + 2 * lines]
    grad_ref, part_ref = refs[9 + 2 * lines : 11 + 2 * lines]
    key_grads, value_grads = refs[11 + 2 * lines :]
    tiles = (heads + 1) // 2
    kv_count = heads // group
    index = pl.program_id(0)
    step = pl.num_programs(0) - 1 - index
    here = pl.multiple_of(step * block, block)
    cosine, sine = cos_ref[...], sin_ref[...]
    lane = lax.broadcasted_iota(jnp.int32, cosine.shape, 1)
    first = lane < 64
    row = lax.broadcasted_iota(jnp.int32, (block, block), 0)
    column = lax.broadcasted_iota(jnp.int32, (block, block), 1)

    @pl.when(index == 0)
    def _():
        key_grads[...] = jnp.zeros_like(key_grads)
        value_grads[...] = jnp.zeros_like(value_grads)

    mixed = line_dot(g_ref[...], out_refs)
    queries, grads, dots = [], [], []
    for head in range(heads):
        tile, side = head // 2, head % 2
        columns = slice(tile * 128, (tile + 1) * 128)
        if side == 0:
            grad_tile = mixed[:, columns].astype(bf16)
            query_tile = q_ref[:, columns]
            products = (grad_tile.astype(f32) * o_ref[:, columns]).T
        mine = first if side == 0 else jnp.logical_not(first)
        queries.append(jnp.where(mine, query_tile, bf16(0)))
        grads.append(jnp.where(mine, grad_tile, bf16(0)))
        dots.append(jnp.sum(products[side * 64 : (side + 1) * 64], axis=0, keepdims=True))
    outs = []
    for start in range(0, heads, together):
        some = range(start, min(start + together, heads))

        def body(j, carry, some=some):
            there = pl.ds(pl.multiple_of(j * block, block), block)
            allowed = row + j * block <= column + here
            after = []
            for head, sofar in zip(some, carry):
                kv = slice(head // group * 128, (head // group + 1) * 128)
                kt = slice(head // group * 64, (head // group + 1) * 64)
                scores = lax.dot_general(
                    k_ref[there, kv], queries[head], transposed, preferred_element_type=f32
                )
                scores = jnp.where(allowed, scores, -1e30)
                weights = jnp.exp(scores - sum_ref[head : head + 1, :])
                back = lax.dot_general(
                    v_ref[there, kv], grads[head], transposed, preferred_element_type=f32
                )
                back = (weights * (back - dots[head])).astype(bf16)
                value_grads[there, kv] += jnp.dot(
                    weights.astype(bf16), grads[head], preferred_element_type=f32
                )
                key_grads[there, kv] += jnp.dot(back, queries[head], preferred_element_type=f32)
                after.append(
                    sofar + jnp.dot(kt_ref[kt, there], back, preferred_element_type=f32)
                )
            return after

        outs += lax.fori_loop(0, step + 1, body, [jnp.zeros((64, block), f32) for _ in some])
    if heads % 2:
        outs.append(jnp.zeros((64, block), f32))
    for tile in range(tiles):
        columns = slice(tile * 128, (tile + 1) * 128)
        both = jnp.concatenate(outs[tile * 2 : tile * 2 + 2], axis=0).T * 0.125
        grad_ref[:, columns] = (both * cosine - half_swap(both) * sine).astype(bf16)
    for kv in range(kv_count):
        columns = slice(kv * 128, (kv + 1) * 128)
        key_grad = key_grads[pl.ds(here, block), columns]
        key_grad = key_grad + pltpu.roll(key_grad, 64, 1)
        key_grad = key_grad * cosine - half_swap(key_grad) * sine
        value_grad = value_grads[pl.ds(here, block), columns]
        value_grad = value_grad + pltpu.roll(value_grad, 64, 1)
        grad_ref[:, (tiles + kv) * 128 : (tiles + kv + 1) * 128] = jnp.where(
            first, key_grad, value_grad
        ).astype(bf16)
    part = part_ref.shape[1] // lines
    for line, ref in enumerate(qkv_refs):
        part_ref[:, line * part : (line + 1) * part] = lax.dot_general(
            grad_ref[...], ref[...], transposed, preferred_element_type=f32
        ).astype(bf16)


def attend_forward(rows, cosine, sine, qkv_lines, out_lines, heads, group, block=256, together=6):
    seq_length, width = rows.shape
    lines = len(qkv_lines)
    tiles, kv_count = (heads + 1) // 2, heads // group
    one = pl.Buffered(1)

    def tall(columns):
        return pl.BlockSpec((block, columns), lambda s: (s, 0))

    def fixed(array):
        return pl.BlockSpec(array.shape, lambda s: (0, 0), pipeline_mode=one)

    wide, narrow = tiles * 128, kv_count * 128
    shapes = [
        ((seq_length, wide), bf16, tall(wide)),
        ((seq_length, narrow), bf16, tall(narrow)),
        ((seq_length, narrow), bf16, tall(narrow)),
        ((narrow // 2, seq_length), bf16, pl.BlockSpec((narrow // 2, block), lambda s: (0, s))),
        ((seq_length, wide), f32, tall(wide)),
        ((seq_length, wide), bf16, tall(wide)),
        ((8, seq_length), f32, pl.BlockSpec((8, block), lambda s: (0, s))),
        ((seq_length, width), bf16, tall(width)),
    ]
    return pl.pallas_call(
        functools.partial(attend_forward_kernel, lines, heads, group, block, together),
        grid=(seq_length // block,),
        in_specs=[tall(width), tall(128), tall(128)] + [fixed(a) for a in qkv_lines + out_lines],
        out_specs=[s[2] for s in shapes],
        out_shape=[jax.ShapeDtypeStruct(s[0], s[1]) for s in shapes],
        scratch_shapes=[
            pltpu.VMEM((seq_length, narrow), bf16),
            pltpu.VMEM((narrow // 2, seq_length), bf16),
        ],
        compiler_params=pltpu.CompilerParams(vmem_limit_bytes=48 * 1024 * 1024),
        cost_estimate=pl.CostEstimate(
            flops=2 * seq_length * width * (2 * wide + 2 * narrow)
            + 4 * heads * seq_length * seq_length * 128,
            bytes_accessed=seq_length * (2 * width * 2 + wide * 8 + narrow * 6),
            transcendentals=heads * seq_length * seq_length,
        ),
        name="attend_forward",
    )(rows, cosine, sine, *qkv_lines, *out_lines)


def attend_backward(grads, cosine, sine, qkv_lines, out_lines, saved, heads, group, block=256, together=6):
    seq_length, width = grads.shape
    lines = len(qkv_lines)
    tiles, kv_count = (heads + 1) // 2, heads // group
    one = pl.Buffered(1)
    last = seq_length // block - 1

    def tall(columns):
        return pl.BlockSpec((block, columns), lambda s: (last - s, 0))

    def fixed(array):
        return pl.BlockSpec(array.shape, lambda s: (0, 0), pipeline_mode=one)

    wide, narrow = tiles * 128, kv_count * 128
    q, k, v, kt, o, sums = saved
    return pl.pallas_call(
        functools.partial(attend_backward_kernel, lines, heads, group, block, together),
        grid=(seq_length // block,),
        in_specs=[tall(width), tall(128), tall(128)]
        + [fixed(a) for a in qkv_lines + out_lines]
        + [
            tall(wide),
            fixed(k),
            fixed(v),
            fixed(kt),
            tall(wide),
            pl.BlockSpec((8, block), lambda s: (0, last - s)),
        ],
        out_specs=[tall(wide + narrow), tall(width)],
        out_shape=[
            jax.ShapeDtypeStruct((seq_length, wide + narrow), bf16),
            jax.ShapeDtypeStruct((seq_length, width), bf16),
        ],
        scratch_shapes=[
            pltpu.VMEM((seq_length, narrow), f32),
            pltpu.VMEM((seq_length, narrow), f32),
        ],
        compiler_params=pltpu.CompilerParams(vmem_limit_bytes=48 * 1024 * 1024),
        cost_estimate=pl.CostEstimate(
            flops=2 * seq_length * width * (2 * wide + 2 * narrow)
            + 8 * heads * seq_length * seq_length * 128,
            bytes_accessed=seq_length * (2 * width * 2 + wide * 10 + narrow * 8),
            transcendentals=heads * seq_length * seq_length,
        ),
        name="attend_backward",
    )(grads, cosine, sine, *qkv_lines, *out_lines, q, k, v, kt, o, sums)


def experts_kernel(sizes, lines, half_ff, experts, row_ref, a_ref, c_ref, router_ref, *refs):
    count = len(sizes) * lines
    weight_refs = refs[:count]
    y_ref, back_ref, act_ref, gate_ref = refs[count:]
    local = sum(sizes)
    width = a_ref.shape[1]
    part = width // lines
    base = row_ref[0] * local
    rows, grads = a_ref[...], c_ref[:, :width]
    chosen = c_ref[:, width:].astype(f32) > 0
    logits = jnp.dot(rows, router_ref[...], preferred_element_type=f32)
    logits = jnp.where(chosen, logits, -1e30)
    top = jnp.max(logits, axis=-1, keepdims=True)
    share = jnp.where(chosen, jnp.exp(logits - top), 0.0)
    share = share / jnp.sum(share, axis=-1, keepdims=True)
    lane = lax.broadcasted_iota(jnp.int32, share.shape, 1)
    dots = jnp.zeros(share.shape, f32)
    index = 0
    for chunk, size in enumerate(sizes):
        refs_here = weight_refs[chunk * lines : (chunk + 1) * lines]
        for member in range(size):
            up = member * 2 * half_ff
            down = size * 2 * half_ff + member * half_ff
            up_out, back = 0.0, 0.0
            for line, ref in enumerate(refs_here):
                columns = slice(line * part, (line + 1) * part)
                up_out = up_out + jnp.dot(
                    rows[:, columns], ref[:, up : up + 2 * half_ff], preferred_element_type=f32
                )
                back = back + jnp.dot(
                    grads[:, columns], ref[:, down : down + half_ff], preferred_element_type=f32
                )
            mine = lane == base + index
            weight = jnp.sum(jnp.where(mine, share, 0.0), axis=-1, keepdims=True)
            gate, upper = up_out[:, :half_ff], up_out[:, half_ff:]
            sigmoid = 1.0 / (1.0 + jnp.exp(-gate))
            silu = gate * sigmoid
            active = (silu * upper).astype(bf16).astype(f32)
            dot = jnp.sum(active * back, axis=-1, keepdims=True)
            high = dot.astype(bf16).astype(f32)
            dots = jnp.where(mine, high, dots)
            dots = jnp.where(lane == base + index + experts, dot - high, dots)
            act_ref[:, index * half_ff : (index + 1) * half_ff] = (weight * active).astype(bf16)
            back = weight * back
            at = index * 2 * half_ff
            gate_ref[:, at : at + half_ff] = (
                back * upper * sigmoid * (1.0 + gate * (1.0 - sigmoid))
            ).astype(bf16)
            gate_ref[:, at + half_ff : at + 2 * half_ff] = (back * silu).astype(bf16)
            index += 1
    for line in range(lines):
        total, total_back, start = 0.0, 0.0, 0
        for chunk, size in enumerate(sizes):
            ref = weight_refs[chunk * lines + line]
            split, stop = size * 2 * half_ff, start + size
            total = total + lax.dot_general(
                act_ref[:, start * half_ff : stop * half_ff],
                ref[:, split:],
                transposed,
                preferred_element_type=f32,
            )
            total_back = total_back + lax.dot_general(
                gate_ref[:, start * 2 * half_ff : stop * 2 * half_ff],
                ref[:, :split],
                transposed,
                preferred_element_type=f32,
            )
            start = stop
        columns = slice(line * part, (line + 1) * part)
        y_ref[:, columns] = total.astype(bf16)
        back_ref[:, columns] = total_back.astype(bf16)
    back_ref[:, width:] = dots.astype(bf16)


def run_experts(row, rows, grads, router, weights, sizes, lines, half_ff, experts, tile=256):
    tall, width = rows.shape
    local = sum(sizes)
    one = pl.Buffered(1)

    def moving(columns):
        return pl.BlockSpec((tile, columns), lambda t, b: (t, 0))

    def fixed(array):
        return pl.BlockSpec(array.shape, lambda t, b: (0, 0), pipeline_mode=one)

    widths = [width, grads.shape[1], local * half_ff, local * 2 * half_ff]
    return pl.pallas_call(
        functools.partial(experts_kernel, sizes, lines, half_ff, experts),
        out_shape=[jax.ShapeDtypeStruct((tall, columns), bf16) for columns in widths],
        grid_spec=pltpu.PrefetchScalarGridSpec(
            num_scalar_prefetch=1,
            grid=(tall // tile,),
            in_specs=[moving(width), moving(grads.shape[1]), fixed(router)]
            + [fixed(w) for w in weights],
            out_specs=[moving(columns) for columns in widths],
        ),
        compiler_params=pltpu.CompilerParams(vmem_limit_bytes=60 * 1024 * 1024),
        cost_estimate=pl.CostEstimate(
            flops=12 * tall * width * half_ff * local,
            bytes_accessed=sum(w.size * 2 for w in weights) + 2 * tall * (sum(widths) + 2 * width),
            transcendentals=tall * half_ff * local,
        ),
        name="run_experts",
    )(row, rows, grads, router, *weights)


def build(mesh):
    seq_size, row_size = mesh.shape["seq"], mesh.shape["row"]
    inner_count = seq_size // outer_count
    outer_groups = [
        [o * inner_count + i for o in range(outer_count)] for i in range(inner_count)
    ]

    def fetch_inner(x, step):
        pairs = []
        for o in range(outer_count):
            for i in range(inner_count):
                pairs.append(
                    (o * inner_count + (i + step) % inner_count, o * inner_count + i)
                )
        return lax.ppermute(x, "seq", pairs)

    def swap_pair(x):
        pairs = []
        for o in range(outer_count):
            for i in range(inner_count):
                pairs.append((o * inner_count + i, (o ^ 1) * inner_count + i))
        return lax.ppermute(x, "seq", pairs)

    def outer_exchange(x):
        return lax.all_to_all(x, "seq", 0, 0, tiled=True, axis_index_groups=outer_groups)

    def gather_weights(pieces):
        line = outer_exchange(pieces)
        lines = [line] + [fetch_inner(line, k) for k in range(1, inner_count)]
        return [each.reshape(-1, pieces.shape[-1]) for each in lines]

    def scatter_grads(grad_of_line, columns):
        arrived = [
            fetch_inner(grad_of_line(k), -k) for k in range(1, inner_count)
        ]
        line = grad_of_line(0).astype(f32)
        for each in arrived:
            line = line + each.astype(f32)
        return outer_exchange(line.astype(bf16).reshape(outer_count, -1, columns))

    def gather_row(x):
        return lax.all_gather(x, "row", axis=0, tiled=True)

    def scatter_row(x):
        return lax.psum_scatter(x, "row", scatter_dimension=0, tiled=True)

    def gather_group(x):
        return gather_row(jnp.concatenate([x, swap_pair(x)], axis=0))

    def scatter_group(x):
        both = scatter_row(x)
        rows = both.shape[0] // pair_count
        return both[:rows].astype(f32) + swap_pair(both[rows:]).astype(f32)

    def sum_all(x):
        for axis, size in (("row", row_size), ("seq", seq_size)):
            distance = 1
            while distance < size:
                x = x + lax.ppermute(x, axis, [(d, d ^ distance) for d in range(size)])
                distance *= 2
        return x

    def on_device(
        tokens,
        routes,
        attn_gain,
        ffn_gain,
        query_weight,
        keyval_weight,
        output_weight,
        router_weight,
        expert_up,
        expert_down,
        cotangent,
    ):
        token_rows, width = tokens.shape
        shard = query_weight.shape[1]
        expert_count = router_weight.shape[2]
        local_experts = expert_up.shape[1]
        expert_width = expert_down.shape[2]
        half_ff = expert_width // pair_count
        head_width = keyval_weight.shape[3] // 2
        local_kv = keyval_weight.shape[2]
        query_columns = query_weight.shape[2]
        keyval_columns = local_kv * 2 * head_width
        heads_local = query_columns // head_width
        group_size = heads_local // local_kv
        seq_index = lax.axis_index("seq")
        row_index = lax.axis_index("row")
        inner = seq_index % inner_count
        parity = (seq_index // inner_count) % pair_count

        def to_basis(x):
            parts = x.reshape(x.shape[0], outer_count, inner_count, shard)
            order = (inner + jnp.arange(inner_count)) % inner_count
            parts = jnp.take(parts, order, axis=2)
            return jnp.swapaxes(parts, 1, 2).reshape(x.shape)

        def from_basis(x):
            parts = x.reshape(x.shape[0], inner_count, outer_count, shard)
            order = (jnp.arange(inner_count) - inner) % inner_count
            parts = jnp.take(parts, order, axis=1)
            return jnp.swapaxes(parts, 1, 2).reshape(x.shape)

        query_pad = -query_columns % 128
        query_wide = query_columns + query_pad
        qkv_columns = query_wide + keyval_columns
        qkv_piece = jnp.concatenate(
            [
                jnp.pad(query_weight[0], ((0, 0), (0, query_pad))),
                keyval_weight[0].reshape(shard, keyval_columns),
            ],
            axis=-1,
        )
        qkv_lines = gather_weights(
            jnp.broadcast_to(qkv_piece, (outer_count,) + qkv_piece.shape)
        )
        hidden = to_basis(tokens.astype(f32))
        gain_attn = to_basis(attn_gain)
        gain_ffn = to_basis(ffn_gain)
        router = to_basis(router_weight[0].T)
        router_wide = jnp.pad(router.T, ((0, 0), (0, 128 - expert_count)))
        cot = to_basis(cotangent)
        attn_scale = inverse_rms(hidden)
        normed = (hidden * attn_scale * gain_attn).astype(bf16)
        normed_all = gather_row(normed)
        seq_length = normed_all.shape[0]

        out_piece = jnp.pad(output_weight[0].T, ((0, 0), (0, query_pad)))
        out_lines = gather_weights(
            jnp.broadcast_to(out_piece, (outer_count,) + out_piece.shape)
        )

        up_parts = expert_up[0].reshape(local_experts, shard, 2, pair_count, half_ff)
        down_parts = jnp.swapaxes(expert_down[0], 1, 2).reshape(
            local_experts, shard, pair_count, half_ff
        )
        chunk_sizes = []
        left = local_experts
        while left > 0:
            chunk_sizes.append(min(2, left))
            left -= chunk_sizes[-1]
        expert_weights = []
        first = 0
        for size in chunk_sizes:
            per_half = []
            for half in range(pair_count):
                ups = up_parts[first : first + size, :, :, half]
                downs = down_parts[first : first + size, :, half]
                ups = jnp.swapaxes(ups, 0, 1).reshape(shard, size * 2 * half_ff)
                downs = jnp.swapaxes(downs, 0, 1).reshape(shard, size * half_ff)
                per_half.append(jnp.concatenate([ups, downs], axis=-1))
            pieces = jnp.stack([per_half[o % pair_count] for o in range(outer_count)])
            expert_weights += gather_weights(pieces)
            first += size

        mask = jnp.sum(
            (routes[0][:, :, None] == jnp.arange(128, dtype=jnp.int32)).astype(f32), axis=1
        )
        cot_all = gather_group(jnp.concatenate([cot, mask.astype(bf16)], axis=-1))

        cosine, sine = rotary_tables(seq_length, head_width)
        cosine = jnp.concatenate([cosine] * 4, axis=-1)
        sine = jnp.concatenate([-sine, sine] * 2, axis=-1)
        q, k, v, kt, attended, attended_low, log_sums, attn_part = attend_forward(
            normed_all, cosine, sine, qkv_lines, out_lines, heads_local, group_size
        )
        attn_out = scatter_row(attn_part).astype(f32)
        after_attn = hidden + attn_out
        ffn_scale = inverse_rms(after_attn)
        normed_moe = (after_attn * ffn_scale * gain_ffn).astype(bf16)
        moe_all = gather_group(normed_moe)

        moe_part, moe_back, weighted, gate_grads = run_experts(
            row_index.astype(jnp.int32)[None],
            moe_all,
            cot_all,
            router_wide,
            expert_weights,
            chunk_sizes,
            inner_count,
            half_ff,
            expert_count,
        )
        returned = scatter_group(moe_back)
        moe_sum = scatter_group(moe_part)
        result = (after_attn + moe_sum).astype(bf16)

        line_width = width // inner_count

        def line_of(x, index):
            return x[:, index * line_width : (index + 1) * line_width]

        def weight_grad(rows, grads):
            return jnp.einsum("td,tf->df", rows, grads, preferred_element_type=f32).astype(bf16)

        expert_grads = []
        first = 0
        for size in chunk_sizes:
            up_grad = gate_grads[:, first * 2 * half_ff : (first + size) * 2 * half_ff]
            active = weighted[:, first * half_ff : (first + size) * half_ff]

            def both(index, up_grad=up_grad, active=active):
                return jnp.concatenate(
                    [
                        weight_grad(line_of(moe_all, index), up_grad),
                        weight_grad(line_of(cot_all, index), active),
                    ],
                    axis=-1,
                )

            expert_grads.append(scatter_grads(both, size * 3 * half_ff))
            first += size

        def mix(rows, chosen):
            logits = jnp.einsum("td,ed->te", rows, router, preferred_element_type=f32)
            logits = jnp.where(chosen > 0, logits, -1e30)
            top = jnp.max(logits, axis=-1, keepdims=True)
            share = jnp.where(chosen > 0, jnp.exp(logits - top), 0.0)
            return share / jnp.sum(share, axis=-1, keepdims=True)

        mixing = mix(normed_moe, mask[:, :expert_count])
        mixing_grad = (
            returned[:, width : width + expert_count]
            + returned[:, width + expert_count : width + 2 * expert_count]
        )
        logit_grad = (
            mixing * (mixing_grad - jnp.sum(mixing * mixing_grad, axis=-1, keepdims=True))
        ).astype(bf16)
        router_part = jnp.einsum("te,td->ed", logit_grad, normed_moe, preferred_element_type=f32)
        normed_moe_grad = returned[:, :width] + jnp.dot(
            logit_grad, router, preferred_element_type=f32
        )
        cot_wide = cot.astype(f32)
        unit = after_attn * ffn_scale
        ffn_part = jnp.sum(normed_moe_grad * unit, axis=0, keepdims=True)
        scaled = normed_moe_grad * gain_ffn
        residual_grad = cot_wide + ffn_scale * (
            scaled - unit * jnp.mean(scaled * unit, axis=-1, keepdims=True)
        )
        branch_all = gather_row(residual_grad.astype(bf16))

        output_got = scatter_grads(
            lambda index: weight_grad(line_of(branch_all, index), attended_low), query_wide
        )
        qkv_grad, normed_part = attend_backward(
            branch_all,
            cosine,
            sine,
            qkv_lines,
            out_lines,
            (q, k, v, kt, attended, log_sums),
            heads_local,
            group_size,
        )
        normed_grad = scatter_row(normed_part).astype(f32)
        qkv_got = scatter_grads(
            lambda index: weight_grad(line_of(normed_all, index), qkv_grad), qkv_columns
        )

        unit = hidden * attn_scale
        attn_part = jnp.sum(normed_grad * unit, axis=0, keepdims=True)
        scaled = normed_grad * gain_attn
        token_grad = residual_grad + attn_scale * (
            scaled - unit * jnp.mean(scaled * unit, axis=-1, keepdims=True)
        )

        early = sum_all(from_basis(jnp.concatenate([router_part, ffn_part], axis=0)))
        late = sum_all(from_basis(attn_part))

        def total(got, start):
            return jnp.sum(got[start::pair_count].astype(f32), axis=0)

        up_out_grads, down_out_grads = [], []
        for size, got in zip(chunk_sizes, expert_grads):
            halves = [total(got, half) for half in range(pair_count)]
            split = size * 2 * half_ff
            ups = jnp.stack(
                [h[:, :split].reshape(shard, size, 2, half_ff) for h in halves], axis=3
            )
            downs = jnp.stack([h[:, split:].reshape(shard, size, half_ff) for h in halves], axis=2)
            up_out_grads.append(
                jnp.swapaxes(ups.reshape(shard, size, 2 * expert_width), 0, 1)
            )
            down_out_grads.append(
                jnp.transpose(downs.reshape(shard, size, expert_width), (1, 2, 0))
            )
        qkv_total = jnp.sum(qkv_got.astype(f32), axis=0)
        output_total = jnp.sum(output_got.astype(f32), axis=0)
        return (
            from_basis(result),
            from_basis(token_grad),
            late,
            early[expert_count:],
            qkv_total[None, :, :query_columns],
            qkv_total[:, query_wide:].reshape(1, shard, local_kv, 2 * head_width),
            output_total.T[None, :query_columns],
            early[:expert_count].T[None],
            jnp.concatenate(up_out_grads, axis=0)[None],
            jnp.concatenate(down_out_grads, axis=0)[None],
        )

    return on_device


def solution(mesh):
    placed = (
        P(("seq", "row"), None),
        P(None, ("seq", "row"), None),
        P(),
        P(),
        P(None, "seq", "row"),
        P(None, "seq", "row", None),
        P(None, "row", "seq"),
        P(),
        P(None, "row", "seq", None),
        P(None, "row", None, "seq"),
        P(("seq", "row"), None),
    )
    return jax.shard_map(
        build(mesh),
        mesh=mesh,
        in_specs=placed,
        out_specs=(
            P(("seq", "row"), None),
            P(("seq", "row"), None),
            P(),
            P(),
            P(None, "seq", "row"),
            P(None, "seq", "row", None),
            P(None, "row", "seq"),
            P(),
            P(None, "row", "seq", None),
            P(None, "row", None, "seq"),
        ),
        check_vma=False,
    )
```
